32 devices in a mesh: pts: 8 (over z, y), grp: 4 (over x, core).
Axes of the slice: x: 2, y: 2, z: 4, core: 2. Of those that a mesh axis runs over, the one named last changes fastest.
Arguments:
- coords: float32 [3, 16384], P(None, ('pts', 'grp')), may hold values from 0 to 1, as said below
- observations: float32 [16384], P(('pts', 'grp')), may hold values from -18 to 18
- length_scales: float32 [3], replicated, may hold values from 0.3 to 1
- nugget: float32 [1], replicated, may hold values from 0.05 to 0.3
- fetch_table: int32 [32, 32, 41], P(('pts', 'grp')), may hold values from 0 to 511
- slot_of: int32 [30, 16384], P(None, ('pts', 'grp')), may hold values from 0 to 2847, as said below
Outputs:
- whitened: float32 [16384], P(('pts', 'grp'))
- neg_loglik: float32 [], replicated
The draws below stay inside these ranges and needn't reach their ends.
Inputs may be any that keep to these rules, and one draw needn't show every extreme that they name: `coords`: the points of the device of tile t and slab s have first coordinate in [t / 8, (t + 1) / 8) and time coordinate in [s / 4, (s + 1) / 4). `slot_of`: the 30 slots of one point are distinct. Slots below 1536 never point before the first tile or after the last one. Only the first 32 points of each device use slots of 1536 or more, and each of those slots is used at most once on its device; on every device some owner's 41 far slots are all used.
All inputs are finite; a program needn't handle non-finite values.
Results may differ from the reference program's by a relative error of at most 0.0003.
Values sent between devices are 32-bit elements; how exact they have to be, the bound alone decides.
No kernel may reach another device: no remote copies, remote signals or barrier semaphores. Data moves between devices by JAX's collectives and lax.ppermute only.
A program may use at most 128 MiB of HBM per device.

```python
import math
import jax
import jax.numpy as jnp
from jax import lax

M = 30
P_DEV = 512
EARLY = 32
OWNERS = 32
NPTS = 16384
FCAP = 41
N_PTS = 8
N_GRP = 4


def draw_coords(key, part):
    device = jnp.arange(NPTS, dtype=jnp.int32) // P_DEV
    tile = (device // N_GRP).astype(jnp.float32)
    slab = (device % N_GRP).astype(jnp.float32)
    spread = jax.random.uniform(jax.random.fold_in(key, 21), (3, NPTS), jnp.float32, 0.0, 1.0)
    first = (tile + spread[0]) / N_PTS
    third = (slab + spread[2]) / N_GRP
    return jnp.stack([first, spread[1], third], axis=0)


def draw_observations(key, part):
    position = jnp.arange(NPTS, dtype=jnp.float32)
    slope = 1.0 + 2.0 * position / NPTS
    rough = jax.random.normal(jax.random.fold_in(key, 12), (NPTS,), jnp.float32)
    return jnp.clip(rough, -6.0, 6.0) * slope


def draw_slot_of(key, part):
    far_total = OWNERS * FCAP
    far_uses = EARLY * M
    series = jnp.arange(far_total, dtype=jnp.int32)
    owner_of = series // FCAP
    stride = P_DEV // (M + 1)

    def per_device(device):
        device_key = jax.random.fold_in(key, device)
        tile = device // N_GRP
        filled = (device + OWNERS // 2) % OWNERS
        noise = jax.random.randint(jax.random.fold_in(device_key, 1), (far_total,), 0, 4096, dtype=jnp.int32)
        score = jnp.where(owner_of == filled, series - far_total, noise * far_total + series)
        chosen = jnp.argsort(score, stable=True)[:far_uses].astype(jnp.int32) + 3 * P_DEV
        chosen = jax.random.permutation(jax.random.fold_in(device_key, 2), chosen)
        chosen = chosen.reshape(EARLY, M).T
        local = jnp.arange(P_DEV, dtype=jnp.int32)[None, :]
        jitter = jax.random.randint(jax.random.fold_in(device_key, 3), (M, P_DEV), 0, stride, dtype=jnp.int32)
        offsets = 1 + jnp.arange(M, dtype=jnp.int32)[:, None] * stride + jitter
        rows = (local + offsets) % P_DEV
        block = jax.random.randint(jax.random.fold_in(device_key, 4), (M, P_DEV), 0, 3, dtype=jnp.int32)
        block = jnp.where((tile == 0) & (block == 0), 1, block)
        block = jnp.where((tile == N_PTS - 1) & (block == 2), 1, block)
        near = block * P_DEV + rows
        return jnp.concatenate([chosen, near[:, EARLY:]], axis=1).astype(jnp.int32)
    blocks = lax.map(per_device, jnp.arange(OWNERS, dtype=jnp.int32))
    return jnp.transpose(blocks, (1, 0, 2)).reshape(M, NPTS)


def touch_ends(result, stream_key, least, high):
    dims = result.shape
    place = [jax.random.randint(jax.random.fold_in(stream_key, axis), (), 0, dims[axis]) for axis in range(len(dims))]
    result = result.at[tuple(place)].set(least)
    longest = dims.index(max(dims))
    place[longest] = (place[longest] + 1) % dims[longest]
    return result.at[tuple(place)].set(high)


def setup_inputs(seed: int = 0) -> dict:
    splits = jax.random.split(jax.random.key(seed), 7)
    coords = draw_coords(jax.random.fold_in(splits[6], 71), 0)
    observations = draw_observations(jax.random.fold_in(splits[6], 71), 0)
    length_scales = jnp.clip(jnp.exp(jax.random.uniform(splits[2], (3,), jnp.float32, math.log(0.3), math.log(1.0))), 0.3, 1.0)
    nugget = jnp.clip(jnp.exp(jax.random.uniform(splits[3], (1,), jnp.float32, math.log(0.05), math.log(0.3))), 0.05, 0.3)
    fetch_table = touch_ends(jax.random.randint(splits[4], (OWNERS, OWNERS, FCAP), 0, P_DEV), jax.random.fold_in(splits[4], 1), 0, P_DEV - 1).astype(jnp.int32)
    slot_of = draw_slot_of(jax.random.fold_in(splits[6], 71), 0)
    return {"coords": coords, "observations": observations, "length_scales": length_scales, "nugget": nugget, "fetch_table": fetch_table, "slot_of": slot_of}


root_three = 1.7320508075688772
half_log_tau = 0.9189385332046727

def covariance(points, inverse_lengths, nugget):
    scaled = points * inverse_lengths[:, None, None]
    gap = scaled[:, :, None, :] - scaled[:, None, :, :]
    distance = jnp.sqrt(lax.optimization_barrier(jnp.sum(gap * gap, axis=0)))
    scaled_distance = root_three * distance
    order = points.shape[1]
    identity = jnp.eye(order, dtype=jnp.float32)[:, :, None]
    return (1.0 + scaled_distance) * jnp.exp(-scaled_distance) + nugget[0] * identity

def eliminate(matrix, values):
    order = matrix.shape[0]
    for step in range(order):
        pivot = jnp.sqrt(matrix[0, 0])
        solved = values[0] / pivot
        if step == order - 1:
            return (solved, pivot)
        column = matrix[1:, 0] / pivot
        matrix = matrix[1:, 1:] - column[:, None, :] * column[None, :, :]
        values = values[1:] - column * solved

def reference(coords, observations, length_scales, nugget, fetch_table, slot_of):
    inverse_lengths = 1.0 / length_scales

    def per_device(device):
        table = lax.dynamic_index_in_dim(fetch_table, device, 0, keepdims=False)
        near_dev = jnp.clip(device + (jnp.arange(3, dtype=jnp.int32) - 1) * N_GRP, 0, OWNERS - 1)
        near_rows = (near_dev[:, None] * P_DEV + jnp.arange(P_DEV, dtype=jnp.int32)[None, :]).reshape(-1)
        far_rows = (jnp.arange(OWNERS, dtype=jnp.int32)[:, None] * P_DEV + table).reshape(-1)
        slot_rows = jnp.concatenate([near_rows, far_rows]).astype(jnp.int32)
        positions = lax.dynamic_slice_in_dim(slot_of, (device * P_DEV).astype(jnp.int32), P_DEV, 1)
        neighbours = slot_rows[positions]
        own_rows = (device * P_DEV + jnp.arange(P_DEV, dtype=jnp.int32))[None, :]
        members = jnp.concatenate([neighbours, own_rows], axis=0)
        points = coords[:, members]
        values = observations[members]
        matrix = covariance(points, inverse_lengths, nugget)
        solved, pivot = eliminate(matrix, values)
        return (solved, jnp.sum(2.0 * jnp.log(pivot) + solved * solved))
    whitened, partial_value = lax.map(per_device, jnp.arange(OWNERS, dtype=jnp.int32))
    neg_loglik = jnp.sum(partial_value) / (2.0 * NPTS) + half_log_tau
    return (whitened.reshape(NPTS), neg_loglik)
```

```python
import functools

import jax
import jax.numpy as jnp
from jax import lax
from jax.experimental import pallas as pl
from jax.experimental.pallas import tpu as pltpu
from jax.sharding import PartitionSpec as P

root_three = 1.7320508075688772
half_log_tau = 0.9189385332046727
LANES = 128
SUBLANES = 8
AXES = ("pts", "grp")


def lane_gather(row, index):
    return jnp.take_along_axis(row, index, axis=1, mode="promise_in_bounds")


def tile_of(ref, row):
    return jnp.broadcast_to(ref[pl.ds(row, 1), :], (SUBLANES, LANES))


def gather_members(all_ref, slot_ref, table_ref, far_index, far_rows, singles, doubles, scales):
    owners, capacity = table_ref.shape
    count, local = slot_ref.shape
    groups = local // LANES
    channels = 4
    rows_each = channels * groups
    near_slots = 3 * local
    tile_id, slab_id = lax.axis_index("pts"), lax.axis_index("grp")
    n_tiles, n_slabs = lax.axis_size("pts"), lax.axis_size("grp")
    device = tile_id * n_slabs + slab_id

    far_index[...] = jnp.zeros(far_index.shape, jnp.int32)
    far_index[:, :capacity] = table_ref[...]
    for base in range(0, owners, SUBLANES):
        index = far_index[base : base + SUBLANES, :]
        lane, chunk = index & (LANES - 1), index >> 7
        for c in range(channels):
            value = None
            for g in range(groups):
                source = all_ref[pl.ds(base * rows_each + c * groups + g, SUBLANES, stride=rows_each), :]
                picked = lane_gather(source, lane)
                value = picked if value is None else jnp.where(chunk == g, picked, value)
            far_rows[c, base : base + SUBLANES, :] = value

    neighbours = [
        jnp.maximum(tile_id - 1, 0) * n_slabs + slab_id,
        device,
        jnp.minimum(tile_id + 1, n_tiles - 1) * n_slabs + slab_id,
    ]
    starts = list(range(0, count - SUBLANES + 1, SUBLANES))
    if starts[-1] + SUBLANES < count:
        starts.append(count - SUBLANES)
    for first in starts:
        slots = [slot_ref[first : first + SUBLANES, g * LANES : (g + 1) * LANES] for g in range(groups)]
        lanes = [s & (LANES - 1) for s in slots]
        chunks = [s >> 7 for s in slots]
        found = [[None] * channels for _ in range(groups)]
        for t in range(3):
            for q in range(groups):
                tables = [tile_of(all_ref, neighbours[t] * rows_each + c * groups + q) for c in range(channels)]
                for g in range(groups):
                    here = chunks[g] == t * groups + q
                    for c in range(channels):
                        picked = lane_gather(tables[c], lanes[g])
                        old = found[g][c]
                        found[g][c] = picked if old is None else jnp.where(here, picked, old)

        far = slots[0] - near_slots

        def one_owner(o, carry):
            place = far - o * capacity
            here = (place >= 0) & (place < capacity)
            lane = place & (LANES - 1)
            return tuple(
                jnp.where(here, lane_gather(tile_of(far_rows.at[c], o), lane), carry[c]) for c in range(channels)
            )

        found[0] = list(lax.fori_loop(0, owners, one_owner, tuple(found[0]), unroll=8))
        for g in range(groups):
            for c in range(channels):
                value = found[g][c]
                if c < 3:
                    value = value * scales[c]
                    singles[c, pl.ds(first * groups + g, SUBLANES, stride=groups), :] = value
                for half in range(2):
                    start = first * SUBLANES + half * groups + g
                    doubles[c, pl.ds(start, SUBLANES, stride=SUBLANES), :] = value
    for c in range(channels):
        own = all_ref[pl.ds(device * rows_each + c * groups, groups), :]
        if c < 3:
            own = own * scales[c][:groups]
            singles[c, count * groups : (count + 1) * groups, :] = own
            singles[c, (count + 1) * groups : (count + 2) * groups, :] = own
        for half in range(2):
            start = count * SUBLANES + half * groups
            doubles[c, start : start + groups, :] = own


def kernel(all_ref, slot_ref, table_ref, lengths, nugget, white_ref, part_ref, far_index, far_rows, singles, doubles, final, scaled):
    count, local = slot_ref.shape
    groups = local // LANES
    order = count + 1
    pairs = (order + 1) // 2
    full = (SUBLANES, LANES)
    scales = [root_three / jnp.full(full, lengths[c], jnp.float32) for c in range(3)]
    gather_members(all_ref, slot_ref, table_ref, far_index, far_rows, singles, doubles, scales)

    low = lax.broadcasted_iota(jnp.int32, full, 0) < groups
    diagonal = jnp.full(full, 1.0 + nugget[0], jnp.float32)

    def single(c, j):
        return singles[c, j * SUBLANES : (j + 1) * SUBLANES, :]

    def double(c, a):
        return doubles[c, a * SUBLANES : (a + 1) * SUBLANES, :]

    def entry(a, j):
        if j == a // 2 and a % 2 == 1:
            return diagonal
        if j == a // 2 and a == order - 1:
            return jnp.where(low, diagonal, double(3, a))
        square = None
        for c in range(3):
            gap = double(c, a) - single(c, j)
            square = gap * gap if square is None else square + gap * gap
        distance = square * lax.rsqrt(jnp.maximum(square, 1e-35))
        value = (1.0 + distance) * jnp.exp(-distance)
        if j == a // 2:
            value = jnp.where(low, diagonal, value)
        if j == pairs - 1:
            value = jnp.where(low, value, double(3, a))
        return value

    def both(value, half):
        other = pltpu.roll(value, groups, 0)
        return jnp.where(low, value, other) if half == 0 else jnp.where(low, other, value)

    def final_at(k, j):
        return pl.ds((k * pairs + j) * SUBLANES, SUBLANES)

    def scaled_at(k, a):
        return pl.ds((k * order + a) * SUBLANES, SUBLANES)

    block, span = 4, 8
    for top in range(0, order, block):
        rows = range(top, min(top + block, order))
        values = {}
        for begin in range(top // 2, pairs, span):
            columns = range(begin, min(begin + span, pairs))
            held = {(a, j): entry(a, j) for a in rows for j in columns if j >= a // 2}
            for k in range(top):
                factors = {a: scaled[scaled_at(k, a), :] for a in rows}
                for j in columns:
                    row = final[final_at(k, j), :]
                    for a in rows:
                        if j >= a // 2:
                            held[a, j] = held[a, j] - factors[a] * row
            for a in rows:
                for k in range(top, a):
                    factor = values[k, a] if (k, a) in values else None
                    if factor is None:
                        factor = both(held[k, a // 2] * values[k], a % 2)
                        values[k, a] = factor
                    for j in columns:
                        if j >= a // 2:
                            held[a, j] = held[a, j] - factor * held[k, j]
                if a not in values:
                    values[a] = 1.0 / both(held[a, a // 2], a % 2)
            for a in rows:
                for j in columns:
                    if j < a // 2:
                        continue
                    value = held[a, j]
                    if a == order - 1:
                        pivot, solved = value, pltpu.roll(value, groups, 0)
                        white = solved * lax.rsqrt(pivot)
                        white_ref[...] = white[:groups]
                        term = jnp.log(pivot) + white * white
                        term = jnp.where(low, term, 0.0)
                        total = jnp.sum(term, axis=0, keepdims=True)
                        part_ref[...] = jnp.broadcast_to(total, part_ref.shape)
                        continue
                    final[final_at(a, j), :] = value
                    times = value * values[a]
                    swapped = pltpu.roll(times, groups, 0)
                    for half in range(2):
                        column = 2 * j + half
                        if top + block <= column < order:
                            pick = jnp.where(low, times, swapped) if half == 0 else jnp.where(low, swapped, times)
                            scaled[scaled_at(a, column), :] = pick


def body(coords, observations, length_scales, nugget, fetch_table, slot_of):
    local = coords.shape[1]
    owners, capacity = fetch_table.shape[1:]
    count = slot_of.shape[0]
    groups = local // LANES
    order = count + 1
    pairs = (order + 1) // 2
    assert 2 * groups == SUBLANES and order % 2 == 1 and capacity <= LANES
    devices = lax.axis_size("pts") * lax.axis_size("grp")
    payload = jnp.concatenate([coords, observations[None, :]], axis=0).reshape(4 * groups, LANES)
    everything = jnp.broadcast_to(payload[None], (devices, 4 * groups, LANES))
    everything = lax.all_to_all(everything, AXES, split_axis=0, concat_axis=0, tiled=True)
    vmem = pl.BlockSpec(memory_space=pltpu.VMEM)
    smem = pl.BlockSpec(memory_space=pltpu.SMEM)
    white, part = pl.pallas_call(
        kernel,
        out_shape=(
            jax.ShapeDtypeStruct((groups, LANES), jnp.float32),
            jax.ShapeDtypeStruct((devices, LANES), jnp.float32),
        ),
        in_specs=[vmem, vmem, vmem, smem, smem],
        out_specs=(vmem, vmem),
        scratch_shapes=[
            pltpu.VMEM((owners, LANES), jnp.int32),
            pltpu.VMEM((4, owners, LANES), jnp.float32),
            pltpu.VMEM((3, pairs * SUBLANES, LANES), jnp.float32),
            pltpu.VMEM((4, order * SUBLANES, LANES), jnp.float32),
            pltpu.VMEM((order * pairs * SUBLANES, LANES), jnp.float32),
            pltpu.VMEM((order * order * SUBLANES, LANES), jnp.float32),
        ],
    )(everything.reshape(devices * 4 * groups, LANES), slot_of, fetch_table[0], length_scales, nugget)
    parts = lax.all_to_all(part, AXES, split_axis=0, concat_axis=0, tiled=True)
    neg_loglik = jnp.sum(parts) / (2.0 * local * devices) + half_log_tau
    return (white.reshape(local), neg_loglik)


def solution(mesh):
    in_specs = (P(None, AXES), P(AXES), P(), P(), P(AXES, None, None), P(None, AXES))
    out_specs = (P(AXES), P())
    return jax.shard_map(body, mesh=mesh, in_specs=in_specs, out_specs=out_specs, check_vma=False)
```

```python
import jax
import jax.numpy as jnp
from jax import lax
from jax.experimental import pallas as pl
from jax.experimental.pallas import tpu as pltpu
from jax.sharding import PartitionSpec as P

root_three = 1.7320508075688772
minus_log2_e = -1.4426950408889634
half_log_tau = 0.9189385332046727
LANES = 128
SUBLANES = 8
CHANNELS = 4
EARLY = 32
AXES = ("pts", "grp")


def lane_gather(row, index):
    return jnp.take_along_axis(row, index, axis=1, mode="promise_in_bounds")


def tile_of(ref, row):
    return jnp.broadcast_to(ref[pl.ds(row, 1), :], (SUBLANES, LANES))


def kernel(all_ref, slot_ref, table_ref, scalars, white_ref, part_ref,
           slots, far_index, far_rows, singles, doubles, final, scaled, inverses):
    owners, capacity = table_ref.shape
    count, local = slot_ref.shape
    groups = local // LANES
    rows_each = CHANNELS * groups
    near_slots = 3 * local
    order = count + 1
    pairs = (order + 1) // 2
    panels = pairs * 2 // SUBLANES
    full = (SUBLANES, LANES)
    tile_id, slab_id = lax.axis_index("pts"), lax.axis_index("grp")
    n_tiles, n_slabs = lax.axis_size("pts"), lax.axis_size("grp")
    device = tile_id * n_slabs + slab_id
    scales = [root_three / jnp.full(full, scalars[c], jnp.float32) for c in range(3)]
    low = lax.broadcasted_iota(jnp.int32, full, 0) < groups
    lane_id = lax.broadcasted_iota(jnp.int32, full, 1)
    diagonal = jnp.full(full, 1.0 + scalars[3], jnp.float32)

    far_index[...] = jnp.zeros(far_index.shape, jnp.int32)
    far_index[:, :capacity] = table_ref[...]
    for base in range(0, owners, SUBLANES):
        index = far_index[base : base + SUBLANES, :]
        lane, chunk = index & (LANES - 1), index >> 7
        for c in range(CHANNELS):
            value = None
            for g in range(groups):
                source = all_ref[pl.ds(base * rows_each + g * CHANNELS + c, SUBLANES, stride=rows_each), :]
                picked = lane_gather(source, lane)
                value = picked if value is None else jnp.where(chunk == g, picked, value)
            far_rows[c, base : base + SUBLANES, :] = value

    slots[count:, :] = jnp.zeros((slots.shape[0] - count, local), jnp.int32)
    slots[:count, :] = slot_ref[...]

    packed = slots[:SUBLANES, :LANES]
    for p in range(1, panels):
        moved = pltpu.roll(slots[p * SUBLANES : (p + 1) * SUBLANES, :LANES], p * EARLY, 1)
        packed = jnp.where(lane_id < p * EARLY, packed, moved)
    place = packed - near_slots
    far = [jnp.zeros(full, jnp.float32)] * CHANNELS
    for o in range(owners):
        here = (place >= 0) & (place < capacity)
        lane = place & (LANES - 1)
        for c in range(CHANNELS):
            far[c] = jnp.where(here, lane_gather(tile_of(far_rows.at[c], o), lane), far[c])
        place = place - capacity

    neighbours = [
        jnp.maximum(tile_id - 1, 0) * n_slabs + slab_id,
        device,
        jnp.minimum(tile_id + 1, n_tiles - 1) * n_slabs + slab_id,
    ]

    def gather(p):
        first = p * SUBLANES
        mine = [slots[first : first + SUBLANES, g * LANES : (g + 1) * LANES] for g in range(groups)]
        lanes = [s & (LANES - 1) for s in mine]
        chunks = [s >> 7 for s in mine]
        found = [[None] * CHANNELS for _ in range(groups)]
        for t in range(3):
            for q in range(groups):
                tables = [tile_of(all_ref, neighbours[t] * rows_each + q * CHANNELS + c) for c in range(CHANNELS)]
                for g in range(groups):
                    here = chunks[g] == t * groups + q
                    for c in range(CHANNELS):
                        picked = lane_gather(tables[c], lanes[g])
                        old = found[g][c]
                        found[g][c] = picked if old is None else jnp.where(here, picked, old)
        distant = mine[0] >= near_slots
        for c in range(CHANNELS):
            moved = pltpu.roll(far[c], LANES - p * EARLY, 1) if p else far[c]
            found[0][c] = jnp.where(distant, moved, found[0][c])
        for g in range(groups):
            for c in range(CHANNELS):
                value = found[g][c]
                if c < 3:
                    value = value * scales[c]
                    singles[c, pl.ds(first * groups + g, SUBLANES, stride=groups), :] = value
                for half in range(2):
                    start = first * SUBLANES + half * groups + g
                    doubles[c, pl.ds(start, SUBLANES, stride=SUBLANES), :] = value
        if p == panels - 1:
            for c in range(CHANNELS):
                own = all_ref[pl.ds(device * rows_each + c, groups, stride=CHANNELS), :]
                if c < 3:
                    own = own * scales[c][:groups]
                    singles[c, count * groups : (count + 1) * groups, :] = own
                for half in range(2):
                    start = count * SUBLANES + half * groups
                    doubles[c, start : start + groups, :] = own

    def single(c, j):
        return singles[c, j * SUBLANES : (j + 1) * SUBLANES, :]

    def double(c, a):
        return doubles[c, a * SUBLANES : (a + 1) * SUBLANES, :]

    def entry(a, j):
        if j == a // 2 and a % 2 == 1:
            return diagonal
        if j == a // 2 and a == order - 1:
            return jnp.where(low, diagonal, double(3, a))
        square = None
        for c in range(3):
            gap = double(c, a) - single(c, j)
            square = gap * gap if square is None else square + gap * gap
        distance = square * lax.rsqrt(jnp.maximum(square, 1e-35))
        value = (1.0 + distance) * jnp.exp2(distance * minus_log2_e)
        if j == a // 2:
            value = jnp.where(low, diagonal, value)
        if j == pairs - 1:
            value = jnp.where(low, value, double(3, a))
        return value

    def halves(value):
        other = pltpu.roll(value, groups, 0)
        return jnp.where(low, value, other), jnp.where(low, other, value)

    def final_at(k, j):
        return pl.ds((k * pairs + j) * SUBLANES, SUBLANES)

    def scaled_at(k, a):
        return pl.ds((k * order + a) * SUBLANES, SUBLANES)

    block = 4

    def eliminate(p):
        columns = range(p * SUBLANES // 2, (p + 1) * SUBLANES // 2)
        start = p * SUBLANES
        for top in range(0, min(start + SUBLANES, order), block):
            rows = range(top, min(top + block, order))
            held = {(a, j): entry(a, j) for a in rows for j in columns if j >= a // 2}
            for k in range(top):
                factors = {a: scaled[scaled_at(k, a), :] for a in rows}
                for j in columns:
                    row = final[final_at(k, j), :]
                    for a in rows:
                        if j >= a // 2:
                            held[a, j] = held[a, j] - factors[a] * row
            made = {}
            for a in rows:
                for k in range(top, a):
                    factor = made[k, a] if (k, a) in made else scaled[scaled_at(k, a), :]
                    for j in columns:
                        if j >= a // 2:
                            held[a, j] = held[a, j] - factor * held[k, j]
                if a == order - 1:
                    pivot = held[a, pairs - 1]
                    white = pltpu.roll(pivot, groups, 0) * lax.rsqrt(pivot)
                    white_ref[...] = white[:groups]
                    term = jnp.where(low, jnp.log(pivot) + white * white, 0.0)
                    total = jnp.sum(term, axis=0, keepdims=True)
                    part_ref[...] = jnp.broadcast_to(total, part_ref.shape)
                    break
                if a >= start:
                    inverse = 1.0 / halves(held[a, a // 2])[a % 2]
                    inverses[a * SUBLANES : (a + 1) * SUBLANES, :] = inverse
                else:
                    inverse = inverses[a * SUBLANES : (a + 1) * SUBLANES, :]
                for j in columns:
                    if j < a // 2:
                        continue
                    final[final_at(a, j), :] = held[a, j]
                    if 2 * j + 1 <= a:
                        continue
                    pair = halves(held[a, j] * inverse)
                    for half in range(2):
                        m = 2 * j + half
                        if a < m < order:
                            made[a, m] = pair[half]
                            scaled[scaled_at(a, m), :] = pair[half]

    gather(0)
    for p in range(panels):
        if p + 1 < panels:
            gather(p + 1)
        eliminate(p)


def body(coords, observations, length_scales, nugget, fetch_table, slot_of):
    local = coords.shape[1]
    owners, capacity = fetch_table.shape[1:]
    count = slot_of.shape[0]
    groups = local // LANES
    order = count + 1
    pairs = (order + 1) // 2
    panels = pairs * 2 // SUBLANES
    assert 2 * groups == SUBLANES and (order + 1) % SUBLANES == 0
    assert capacity <= LANES and panels * EARLY <= LANES
    devices = lax.axis_size("pts") * lax.axis_size("grp")
    payload = jnp.concatenate([coords, observations[None, :]], axis=0)
    everything = jnp.broadcast_to(payload[None], (devices, CHANNELS, local))
    everything = lax.all_to_all(everything, AXES, split_axis=0, concat_axis=0, tiled=True)
    everything = everything.reshape(devices, CHANNELS, groups, LANES).transpose(0, 2, 1, 3)
    scalars = jnp.concatenate([length_scales, nugget])
    vmem = pl.BlockSpec(memory_space=pltpu.VMEM)
    smem = pl.BlockSpec(memory_space=pltpu.SMEM)
    white, part = pl.pallas_call(
        kernel,
        out_shape=(
            jax.ShapeDtypeStruct((groups, LANES), jnp.float32),
            jax.ShapeDtypeStruct((devices, LANES), jnp.float32),
        ),
        in_specs=[vmem, vmem, vmem, smem],
        out_specs=(vmem, vmem),
        scratch_shapes=[
            pltpu.VMEM((panels * SUBLANES, local), jnp.int32),
            pltpu.VMEM((owners, LANES), jnp.int32),
            pltpu.VMEM((CHANNELS, owners, LANES), jnp.float32),
            pltpu.VMEM((3, pairs * SUBLANES, LANES), jnp.float32),
            pltpu.VMEM((CHANNELS, 2 * pairs * SUBLANES, LANES), jnp.float32),
            pltpu.VMEM((order * pairs * SUBLANES, LANES), jnp.float32),
            pltpu.VMEM((order * order * SUBLANES, LANES), jnp.float32),
            pltpu.VMEM((order * SUBLANES, LANES), jnp.float32),
        ],
        compiler_params=pltpu.CompilerParams(vmem_limit_bytes=16 << 20),
    )(everything.reshape(devices * CHANNELS * groups, LANES), slot_of, fetch_table[0], scalars)
    parts = lax.all_to_all(part, AXES, split_axis=0, concat_axis=0, tiled=True)
    neg_loglik = jnp.sum(parts) / (2.0 * local * devices) + half_log_tau
    return (white.reshape(local), neg_loglik)


def solution(mesh):
    in_specs = (P(None, AXES), P(AXES), P(), P(), P(AXES, None, None), P(None, AXES))
    out_specs = (P(AXES), P())
    return jax.shard_map(body, mesh=mesh, in_specs=in_specs, out_specs=out_specs, check_vma=False)
```

```python
import jax
import jax.numpy as jnp
from jax import lax
from jax.experimental import pallas as pl
from jax.experimental.pallas import tpu as pltpu
from jax.sharding import PartitionSpec as P

root_three = 1.7320508075688772
minus_log2_e = -1.4426950408889634
half_log_tau = 0.9189385332046727
LANES = 128
SUBLANES = 8
CHANNELS = 4
EARLY = 32
AXES = ("pts", "grp")


def lane_gather(row, index):
    return jnp.take_along_axis(row, index, axis=1, mode="promise_in_bounds")


def tile_of(ref, row):
    return jnp.broadcast_to(ref[pl.ds(row, 1), :], (SUBLANES, LANES))


def kernel(all_ref, slot_ref, table_ref, scalars, white_ref, part_ref,
           slots, far_index, far_rows, singles, doubles, final, scaled, inverses):
    owners, capacity = table_ref.shape
    count, local = slot_ref.shape
    groups = local // LANES
    rows_each = CHANNELS * groups
    near_slots = 3 * local
    order = count + 1
    pairs = (order + 1) // 2
    panels = pairs * 2 // SUBLANES
    full = (SUBLANES, LANES)
    tile_id, slab_id = lax.axis_index("pts"), lax.axis_index("grp")
    n_tiles, n_slabs = lax.axis_size("pts"), lax.axis_size("grp")
    device = tile_id * n_slabs + slab_id
    scales = [root_three / jnp.broadcast_to(scalars[:, c : c + 1], full) for c in range(3)]
    low = lax.broadcasted_iota(jnp.int32, full, 0) < groups
    lane_id = lax.broadcasted_iota(jnp.int32, full, 1)
    diagonal = 1.0 + jnp.broadcast_to(scalars[:, 3:4], full)

    far_index[...] = jnp.zeros(far_index.shape, jnp.int32)
    far_index[:, :capacity] = table_ref[...]
    for base in range(0, owners, SUBLANES):
        index = far_index[base : base + SUBLANES, :]
        lane, chunk = index & (LANES - 1), index >> 7
        for c in range(CHANNELS):
            value = None
            for g in range(groups):
                source = all_ref[pl.ds(base * rows_each + g * CHANNELS + c, SUBLANES, stride=rows_each), :]
                picked = lane_gather(source, lane)
                value = picked if value is None else jnp.where(chunk == g, picked, value)
            far_rows[c, base : base + SUBLANES, :] = value

    slots[count:, :] = jnp.zeros((slots.shape[0] - count, local), jnp.int32)
    slots[:count, :] = slot_ref[...]

    packed = slots[:SUBLANES, :LANES]
    for p in range(1, panels):
        moved = pltpu.roll(slots[p * SUBLANES : (p + 1) * SUBLANES, :LANES], p * EARLY, 1)
        packed = jnp.where(lane_id < p * EARLY, packed, moved)
    place = packed - near_slots
    far = [jnp.zeros(full, jnp.float32)] * CHANNELS
    for o in range(owners):
        here = (place >= 0) & (place < capacity)
        lane = place & (LANES - 1)
        for c in range(CHANNELS):
            far[c] = jnp.where(here, lane_gather(tile_of(far_rows.at[c], o), lane), far[c])
        place = place - capacity

    neighbours = [
        jnp.maximum(tile_id - 1, 0) * n_slabs + slab_id,
        device,
        jnp.minimum(tile_id + 1, n_tiles - 1) * n_slabs + slab_id,
    ]

    def gather(p, g):
        first = p * SUBLANES
        mine = slots[first : first + SUBLANES, g * LANES : (g + 1) * LANES]
        lane, chunk = mine & (LANES - 1), mine >> 7
        found = [None] * CHANNELS
        for t in range(3):
            for q in range(groups):
                here = chunk == t * groups + q
                for c in range(CHANNELS):
                    picked = lane_gather(tile_of(all_ref, neighbours[t] * rows_each + q * CHANNELS + c), lane)
                    found[c] = picked if found[c] is None else jnp.where(here, picked, found[c])
        if g == 0:
            distant = mine >= near_slots
            for c in range(CHANNELS):
                moved = pltpu.roll(far[c], LANES - p * EARLY, 1) if p else far[c]
                found[c] = jnp.where(distant, moved, found[c])
        for c in range(CHANNELS):
            value = found[c]
            if c < 3:
                value = value * scales[c]
                singles[c, pl.ds(first * groups + g, SUBLANES, stride=groups), :] = value
            for half in range(2):
                start = first * SUBLANES + half * groups + g
                doubles[c, pl.ds(start, SUBLANES, stride=SUBLANES), :] = value
        if p == panels - 1 and g == groups - 1:
            for c in range(CHANNELS):
                own = all_ref[pl.ds(device * rows_each + c, groups, stride=CHANNELS), :]
                if c < 3:
                    own = own * scales[c][:groups]
                    singles[c, count * groups : (count + 1) * groups, :] = own
                for half in range(2):
                    start = count * SUBLANES + half * groups
                    doubles[c, start : start + groups, :] = own

    def single(c, j):
        return singles[c, j * SUBLANES : (j + 1) * SUBLANES, :]

    def double(c, a):
        return doubles[c, a * SUBLANES : (a + 1) * SUBLANES, :]

    def entry(a, j):
        if j == a // 2 and a % 2 == 1:
            return diagonal
        if j == a // 2 and a == order - 1:
            return jnp.where(low, diagonal, double(3, a))
        square = None
        for c in range(3):
            gap = double(c, a) - single(c, j)
            square = gap * gap if square is None else square + gap * gap
        distance = square * lax.rsqrt(jnp.maximum(square, 1e-35))
        value = (1.0 + distance) * jnp.exp2(distance * minus_log2_e)
        if j == a // 2:
            value = jnp.where(low, diagonal, value)
        if j == pairs - 1:
            value = jnp.where(low, value, double(3, a))
        return value

    def halves(value):
        other = pltpu.roll(value, groups, 0)
        return jnp.where(low, value, other), jnp.where(low, other, value)

    def final_at(k, j):
        return pl.ds((k * pairs + j) * SUBLANES, SUBLANES)

    def scaled_at(k, a):
        return pl.ds((k * order + a) * SUBLANES, SUBLANES)

    block = 4

    def eliminate(p, waiting):
        columns = range(p * SUBLANES // 2, (p + 1) * SUBLANES // 2)
        start = p * SUBLANES
        tops = range(0, min(start + SUBLANES, order), block)
        for step, top in enumerate(tops):
            for part in waiting[step * len(waiting) // len(tops) : (step + 1) * len(waiting) // len(tops)]:
                gather(*part)
            rows = range(top, min(top + block, order))
            held = {(a, j): entry(a, j) for a in rows for j in columns if j >= a // 2}
            for k in range(top):
                factors = {a: scaled[scaled_at(k, a), :] for a in rows}
                for j in columns:
                    row = final[final_at(k, j), :]
                    for a in rows:
                        if j >= a // 2:
                            held[a, j] = held[a, j] - factors[a] * row
            made = {}
            for a in rows:
                for k in range(top, a):
                    factor = made[k, a] if (k, a) in made else scaled[scaled_at(k, a), :]
                    for j in columns:
                        if j >= a // 2:
                            held[a, j] = held[a, j] - factor * held[k, j]
                if a == order - 1:
                    pivot = held[a, pairs - 1]
                    white = pltpu.roll(pivot, groups, 0) * lax.rsqrt(pivot)
                    white_ref[...] = white[:groups]
                    term = jnp.where(low, jnp.log(pivot) + white * white, 0.0)
                    total = jnp.sum(term, axis=0, keepdims=True)
                    part_ref[...] = jnp.broadcast_to(total, part_ref.shape)
                    break
                if a >= start:
                    inverse = 1.0 / halves(held[a, a // 2])[a % 2]
                    inverses[a * SUBLANES : (a + 1) * SUBLANES, :] = inverse
                else:
                    inverse = inverses[a * SUBLANES : (a + 1) * SUBLANES, :]
                for j in columns:
                    if j < a // 2:
                        continue
                    final[final_at(a, j), :] = held[a, j]
                    if 2 * j + 1 <= a:
                        continue
                    pair = halves(held[a, j] * inverse)
                    for half in range(2):
                        m = 2 * j + half
                        if a < m < order:
                            made[a, m] = pair[half]
                            scaled[scaled_at(a, m), :] = pair[half]

    for g in range(groups):
        gather(0, g)
    for p in range(panels):
        eliminate(p, [(p + 1, g) for g in range(groups)] if p + 1 < panels else [])


def body(coords, observations, length_scales, nugget, fetch_table, slot_of):
    local = coords.shape[1]
    owners, capacity = fetch_table.shape[1:]
    count = slot_of.shape[0]
    groups = local // LANES
    order = count + 1
    pairs = (order + 1) // 2
    panels = pairs * 2 // SUBLANES
    assert 2 * groups == SUBLANES and (order + 1) % SUBLANES == 0
    assert capacity <= LANES and panels * EARLY <= LANES
    devices = lax.axis_size("pts") * lax.axis_size("grp")
    payload = jnp.concatenate([coords, observations[None, :]], axis=0)
    everything = jnp.broadcast_to(payload[None], (devices, CHANNELS, local))
    everything = lax.all_to_all(everything, AXES, split_axis=0, concat_axis=0, tiled=True)
    everything = everything.reshape(devices, CHANNELS, groups, LANES).transpose(0, 2, 1, 3)
    scalars = jnp.concatenate([length_scales, nugget])[None]
    vmem = pl.BlockSpec(memory_space=pltpu.VMEM)
    white, part = pl.pallas_call(
        kernel,
        out_shape=(
            jax.ShapeDtypeStruct((groups, LANES), jnp.float32),
            jax.ShapeDtypeStruct((devices, LANES), jnp.float32),
        ),
        in_specs=[vmem, vmem, vmem, vmem],
        out_specs=(vmem, vmem),
        scratch_shapes=[
            pltpu.VMEM((panels * SUBLANES, local), jnp.int32),
            pltpu.VMEM((owners, LANES), jnp.int32),
            pltpu.VMEM((CHANNELS, owners, LANES), jnp.float32),
            pltpu.VMEM((3, pairs * SUBLANES, LANES), jnp.float32),
            pltpu.VMEM((CHANNELS, 2 * pairs * SUBLANES, LANES), jnp.float32),
            pltpu.VMEM((order * pairs * SUBLANES, LANES), jnp.float32),
            pltpu.VMEM((order * order * SUBLANES, LANES), jnp.float32),
            pltpu.VMEM((order * SUBLANES, LANES), jnp.float32),
        ],
        compiler_params=pltpu.CompilerParams(vmem_limit_bytes=16 << 20),
    )(everything.reshape(devices * CHANNELS * groups, LANES), slot_of, fetch_table[0], scalars)
    parts = lax.all_to_all(part, AXES, split_axis=0, concat_axis=0, tiled=True)
    neg_loglik = jnp.sum(parts) / (2.0 * local * devices) + half_log_tau
    return (white.reshape(local), neg_loglik)


def solution(mesh):
    in_specs = (P(None, AXES), P(AXES), P(), P(), P(AXES, None, None), P(None, AXES))
    out_specs = (P(AXES), P())
    return jax.shard_map(body, mesh=mesh, in_specs=in_specs, out_specs=out_specs, check_vma=False)
```

```python
import jax
import jax.numpy as jnp
from jax import lax
from jax.experimental import pallas as pl
from jax.experimental.pallas import tpu as pltpu
from jax.sharding import PartitionSpec as P

root_three = 1.7320508075688772
minus_log2_e = -1.4426950408889634
half_log_tau = 0.9189385332046727
LANES = 128
SUBLANES = 8
CHANNELS = 4
EARLY = 32
AXES = ("pts", "grp")


def lane_gather(row, index):
    return jnp.take_along_axis(row, index, axis=1, mode="promise_in_bounds")


def tile_of(ref, row):
    return jnp.broadcast_to(ref[pl.ds(row, 1), :], (SUBLANES, LANES))


def kernel(same_ref, other_ref, slot_ref, table_ref, scalars, white_ref, part_ref,
           slots, far_index, far_rows, singles, doubles, final, scaled, inverses):
    owners, capacity = table_ref.shape
    count, local = slot_ref.shape
    groups = local // LANES
    rows_each = CHANNELS * groups
    near_slots = 3 * local
    order = count + 1
    pairs = (order + 1) // 2
    panels = pairs * 2 // SUBLANES
    full = (SUBLANES, LANES)
    tile_id, slab_id = lax.axis_index("pts"), lax.axis_index("grp")
    n_tiles, n_slabs = lax.axis_size("pts"), lax.axis_size("grp")
    device = tile_id * n_slabs + slab_id
    scales = [root_three / jnp.broadcast_to(scalars[:, c : c + 1], full) for c in range(3)]
    low = lax.broadcasted_iota(jnp.int32, full, 0) < groups
    lane_id = lax.broadcasted_iota(jnp.int32, full, 1)
    diagonal = 1.0 + jnp.broadcast_to(scalars[:, 3:4], full)

    far_index[...] = jnp.zeros(far_index.shape, jnp.int32)
    far_index[:, :capacity] = table_ref[...]
    parity = device % 2
    for first, ref, base in [
        (start, ref, base)
        for start, ref in ((parity, same_ref), (1 - parity, other_ref))
        for base in range(0, owners // 2, SUBLANES)
    ]:
        theirs = pl.ds(first + 2 * base, SUBLANES, stride=2)
        index = far_index[theirs, :]
        lane, chunk = index & (LANES - 1), index >> 7
        for c in range(CHANNELS):
            value = None
            for g in range(groups):
                source = ref[pl.ds(base * rows_each + g * CHANNELS + c, SUBLANES, stride=rows_each), :]
                picked = lane_gather(source, lane)
                value = picked if value is None else jnp.where(chunk == g, picked, value)
            far_rows[c, theirs, :] = value

    slots[count:, :] = jnp.zeros((slots.shape[0] - count, local), jnp.int32)
    slots[:count, :] = slot_ref[...]

    packed = slots[:SUBLANES, :LANES]
    for p in range(1, panels):
        moved = pltpu.roll(slots[p * SUBLANES : (p + 1) * SUBLANES, :LANES], p * EARLY, 1)
        packed = jnp.where(lane_id < p * EARLY, packed, moved)
    place = packed - near_slots
    far = [jnp.zeros(full, jnp.float32)] * CHANNELS
    for o in range(owners):
        here = (place >= 0) & (place < capacity)
        lane = place & (LANES - 1)
        for c in range(CHANNELS):
            far[c] = jnp.where(here, lane_gather(tile_of(far_rows.at[c], o), lane), far[c])
        place = place - capacity

    neighbours = [
        (jnp.maximum(tile_id - 1, 0) * n_slabs + slab_id) // 2,
        device // 2,
        (jnp.minimum(tile_id + 1, n_tiles - 1) * n_slabs + slab_id) // 2,
    ]

    def gather(p, g):
        first = p * SUBLANES
        mine = slots[first : first + SUBLANES, g * LANES : (g + 1) * LANES]
        lane, chunk = mine & (LANES - 1), mine >> 7
        found = [None] * CHANNELS
        for t in range(3):
            for q in range(groups):
                here = chunk == t * groups + q
                for c in range(CHANNELS):
                    picked = lane_gather(tile_of(same_ref, neighbours[t] * rows_each + q * CHANNELS + c), lane)
                    found[c] = picked if found[c] is None else jnp.where(here, picked, found[c])
        if g == 0:
            distant = mine >= near_slots
            for c in range(CHANNELS):
                moved = pltpu.roll(far[c], LANES - p * EARLY, 1) if p else far[c]
                found[c] = jnp.where(distant, moved, found[c])
        for c in range(CHANNELS):
            value = found[c]
            if c < 3:
                value = value * scales[c]
                singles[c, pl.ds(first * groups + g, SUBLANES, stride=groups), :] = value
            for half in range(2):
                start = first * SUBLANES + half * groups + g
                doubles[c, pl.ds(start, SUBLANES, stride=SUBLANES), :] = value
        if p == panels - 1 and g == groups - 1:
            for c in range(CHANNELS):
                own = same_ref[pl.ds(device // 2 * rows_each + c, groups, stride=CHANNELS), :]
                if c < 3:
                    own = own * scales[c][:groups]
                    singles[c, count * groups : (count + 1) * groups, :] = own
                for half in range(2):
                    start = count * SUBLANES + half * groups
                    doubles[c, start : start + groups, :] = own

    def single(c, j):
        return singles[c, j * SUBLANES : (j + 1) * SUBLANES, :]

    def double(c, a):
        return doubles[c, a * SUBLANES : (a + 1) * SUBLANES, :]

    def entry(a, j):
        if j == a // 2 and a % 2 == 1:
            return diagonal
        if j == a // 2 and a == order - 1:
            return jnp.where(low, diagonal, double(3, a))
        square = None
        for c in range(3):
            gap = double(c, a) - single(c, j)
            square = gap * gap if square is None else square + gap * gap
        distance = square * lax.rsqrt(jnp.maximum(square, 1e-35))
        value = (1.0 + distance) * jnp.exp2(distance * minus_log2_e)
        if j == a // 2:
            value = jnp.where(low, diagonal, value)
        if j == pairs - 1:
            value = jnp.where(low, value, double(3, a))
        return value

    def halves(value):
        other = pltpu.roll(value, groups, 0)
        return jnp.where(low, value, other), jnp.where(low, other, value)

    def final_at(k, j):
        return pl.ds((k * pairs + j) * SUBLANES, SUBLANES)

    def scaled_at(k, a):
        return pl.ds((k * order + a) * SUBLANES, SUBLANES)

    block = 4

    def eliminate(p, waiting):
        columns = range(p * SUBLANES // 2, (p + 1) * SUBLANES // 2)
        start = p * SUBLANES
        tops = range(0, min(start + SUBLANES, order), block)
        for step, top in enumerate(tops):
            for part in waiting[step * len(waiting) // len(tops) : (step + 1) * len(waiting) // len(tops)]:
                gather(*part)
            rows = range(top, min(top + block, order))
            held = {(a, j): entry(a, j) for a in rows for j in columns if j >= a // 2}
            for k in range(top):
                factors = {a: scaled[scaled_at(k, a), :] for a in rows}
                for j in columns:
                    row = final[final_at(k, j), :]
                    for a in rows:
                        if j >= a // 2:
                            held[a, j] = held[a, j] - factors[a] * row
            made = {}
            for a in rows:
                for k in range(top, a):
                    factor = made[k, a] if (k, a) in made else scaled[scaled_at(k, a), :]
                    for j in columns:
                        if j >= a // 2:
                            held[a, j] = held[a, j] - factor * held[k, j]
                if a == order - 1:
                    pivot = held[a, pairs - 1]
                    white = pltpu.roll(pivot, groups, 0) * lax.rsqrt(pivot)
                    white_ref[...] = white[:groups]
                    term = jnp.where(low, jnp.log(pivot) + white * white, 0.0)
                    total = jnp.sum(term, axis=0, keepdims=True)
                    part_ref[...] = jnp.broadcast_to(total, part_ref.shape)
                    break
                if a >= start:
                    inverse = 1.0 / halves(held[a, a // 2])[a % 2]
                    inverses[a * SUBLANES : (a + 1) * SUBLANES, :] = inverse
                else:
                    inverse = inverses[a * SUBLANES : (a + 1) * SUBLANES, :]
                for j in columns:
                    if j < a // 2:
                        continue
                    final[final_at(a, j), :] = held[a, j]
                    if 2 * j + 1 <= a:
                        continue
                    pair = halves(held[a, j] * inverse)
                    for half in range(2):
                        m = 2 * j + half
                        if a < m < order:
                            made[a, m] = pair[half]
                            scaled[scaled_at(a, m), :] = pair[half]

    for g in range(groups):
        gather(0, g)
    for p in range(panels):
        eliminate(p, [(p + 1, g) for g in range(groups)] if p + 1 < panels else [])


def body(coords, observations, length_scales, nugget, fetch_table, slot_of):
    local = coords.shape[1]
    owners, capacity = fetch_table.shape[1:]
    count = slot_of.shape[0]
    groups = local // LANES
    order = count + 1
    pairs = (order + 1) // 2
    panels = pairs * 2 // SUBLANES
    assert 2 * groups == SUBLANES and (order + 1) % SUBLANES == 0
    assert capacity <= LANES and panels * EARLY <= LANES
    devices = lax.axis_size("pts") * lax.axis_size("grp")
    payload = jnp.concatenate([coords, observations[None, :]], axis=0)
    n_slabs = lax.axis_size("grp")
    assert n_slabs % 2 == 0 and devices % (2 * SUBLANES) == 0
    alike = [[d for d in range(devices) if d % 2 == parity] for parity in range(2)]
    same = jnp.broadcast_to(payload[None], (devices // 2, CHANNELS, local))
    same = lax.all_to_all(same, AXES, split_axis=0, concat_axis=0, tiled=True, axis_index_groups=alike)
    same, length_scales, nugget = lax.optimization_barrier((same, length_scales, nugget))
    other = lax.ppermute(same, "grp", [(i, i ^ 1) for i in range(n_slabs)])

    def rows(received):
        received = received.reshape(devices // 2, CHANNELS, groups, LANES).transpose(0, 2, 1, 3)
        return received.reshape(devices // 2 * CHANNELS * groups, LANES)

    scalars = jnp.concatenate([length_scales, nugget])[None]
    vmem = pl.BlockSpec(memory_space=pltpu.VMEM)
    white, part = pl.pallas_call(
        kernel,
        out_shape=(
            jax.ShapeDtypeStruct((groups, LANES), jnp.float32),
            jax.ShapeDtypeStruct((devices, LANES), jnp.float32),
        ),
        in_specs=[vmem] * 5,
        out_specs=(vmem, vmem),
        scratch_shapes=[
            pltpu.VMEM((panels * SUBLANES, local), jnp.int32),
            pltpu.VMEM((owners, LANES), jnp.int32),
            pltpu.VMEM((CHANNELS, owners, LANES), jnp.float32),
            pltpu.VMEM((3, pairs * SUBLANES, LANES), jnp.float32),
            pltpu.VMEM((CHANNELS, 2 * pairs * SUBLANES, LANES), jnp.float32),
            pltpu.VMEM((order * pairs * SUBLANES, LANES), jnp.float32),
            pltpu.VMEM((order * order * SUBLANES, LANES), jnp.float32),
            pltpu.VMEM((order * SUBLANES, LANES), jnp.float32),
        ],
        compiler_params=pltpu.CompilerParams(vmem_limit_bytes=16 << 20),
    )(rows(same), rows(other), slot_of, fetch_table[0], scalars)
    parts = lax.all_to_all(part, AXES, split_axis=0, concat_axis=0, tiled=True)
    neg_loglik = jnp.sum(parts) / (2.0 * local * devices) + half_log_tau
    return (white.reshape(local), neg_loglik)


def solution(mesh):
    in_specs = (P(None, AXES), P(AXES), P(), P(), P(AXES, None, None), P(None, AXES))
    out_specs = (P(AXES), P())
    return jax.shard_map(body, mesh=mesh, in_specs=in_specs, out_specs=out_specs, check_vma=False)
```

```python
import jax
import jax.numpy as jnp
from jax import lax
from jax.experimental import pallas as pl
from jax.experimental.pallas import tpu as pltpu
from jax.sharding import PartitionSpec as P

root_three = 1.7320508075688772
minus_log2_e = -1.4426950408889634
half_log_tau = 0.9189385332046727
LANES = 128
SUBLANES = 8
CHANNELS = 4
EARLY = 32
AXES = ("pts", "grp")


def lane_gather(row, index):
    return jnp.take_along_axis(row, index, axis=1, mode="promise_in_bounds")


def tile_of(ref, row):
    return jnp.broadcast_to(ref[pl.ds(row, 1), :], (SUBLANES, LANES))


def kernel(same_ref, other_ref, slot_ref, table_ref, scalars, white_ref, part_ref,
           slots, far_index, far_rows, singles, doubles, final, scaled, inverses):
    owners, capacity = table_ref.shape
    count, local = slot_ref.shape
    groups = local // LANES
    rows_each = CHANNELS * groups
    near_slots = 3 * local
    order = count + 1
    pairs = (order + 1) // 2
    panels = pairs * 2 // SUBLANES
    full = (SUBLANES, LANES)
    tile_id, slab_id = lax.axis_index("pts"), lax.axis_index("grp")
    n_tiles, n_slabs = lax.axis_size("pts"), lax.axis_size("grp")
    device = tile_id * n_slabs + slab_id
    scales = [root_three / jnp.broadcast_to(scalars[:, c : c + 1], full) for c in range(3)]
    low = lax.broadcasted_iota(jnp.int32, full, 0) < groups
    lane_id = lax.broadcasted_iota(jnp.int32, full, 1)
    diagonal = 1.0 + jnp.broadcast_to(scalars[:, 3:4], full)

    far_index[...] = jnp.zeros(far_index.shape, jnp.int32)
    far_index[:, :capacity] = table_ref[...]
    parity = device % 2
    for first, ref, base in [
        (start, ref, base)
        for start, ref in ((parity, same_ref), (1 - parity, other_ref))
        for base in range(0, owners // 2, SUBLANES)
    ]:
        theirs = pl.ds(first + 2 * base, SUBLANES, stride=2)
        index = far_index[theirs, :]
        lane, chunk = index & (LANES - 1), index >> 7
        for c in range(CHANNELS):
            value = None
            for g in range(groups):
                source = ref[pl.ds(base * rows_each + g * CHANNELS + c, SUBLANES, stride=rows_each), :]
                picked = lane_gather(source, lane)
                value = picked if value is None else jnp.where(chunk == g, picked, value)
            far_rows[c, theirs, :] = value

    slots[count:, :] = jnp.zeros((slots.shape[0] - count, local), jnp.int32)
    slots[:count, :] = slot_ref[...]

    packed = slots[:SUBLANES, :LANES]
    for p in range(1, panels):
        moved = pltpu.roll(slots[p * SUBLANES : (p + 1) * SUBLANES, :LANES], p * EARLY, 1)
        packed = jnp.where(lane_id < p * EARLY, packed, moved)
    place = packed - near_slots
    far = [jnp.zeros(full, jnp.float32)] * CHANNELS
    for o in range(owners):
        here = (place >= 0) & (place < capacity)
        lane = place & (LANES - 1)
        for c in range(CHANNELS):
            far[c] = jnp.where(here, lane_gather(tile_of(far_rows.at[c], o), lane), far[c])
        place = place - capacity

    neighbours = [
        (jnp.maximum(tile_id - 1, 0) * n_slabs + slab_id) // 2,
        device // 2,
        (jnp.minimum(tile_id + 1, n_tiles - 1) * n_slabs + slab_id) // 2,
    ]

    def gather(p, g):
        first = p * SUBLANES
        mine = slots[first : first + SUBLANES, g * LANES : (g + 1) * LANES]
        lane, chunk = mine & (LANES - 1), mine >> 7
        found = [None] * CHANNELS
        for t in range(3):
            for q in range(groups):
                here = chunk == t * groups + q
                for c in range(CHANNELS):
                    picked = lane_gather(tile_of(same_ref, neighbours[t] * rows_each + q * CHANNELS + c), lane)
                    found[c] = picked if found[c] is None else jnp.where(here, picked, found[c])
        if g == 0:
            distant = mine >= near_slots
            for c in range(CHANNELS):
                moved = pltpu.roll(far[c], LANES - p * EARLY, 1) if p else far[c]
                found[c] = jnp.where(distant, moved, found[c])
        for c in range(CHANNELS):
            value = found[c]
            if c < 3:
                value = value * scales[c]
                singles[c, pl.ds(first * groups + g, SUBLANES, stride=groups), :] = value
            for half in range(2):
                start = first * SUBLANES + half * groups + g
                doubles[c, pl.ds(start, SUBLANES, stride=SUBLANES), :] = value
        if p == panels - 1 and g == groups - 1:
            for c in range(CHANNELS):
                own = same_ref[pl.ds(device // 2 * rows_each + c, groups, stride=CHANNELS), :]
                if c < 3:
                    own = own * scales[c][:groups]
                    singles[c, count * groups : (count + 1) * groups, :] = own
                for half in range(2):
                    start = count * SUBLANES + half * groups
                    doubles[c, start : start + groups, :] = own

    def single(c, j):
        return singles[c, j * SUBLANES : (j + 1) * SUBLANES, :]

    def double(c, a):
        return doubles[c, a * SUBLANES : (a + 1) * SUBLANES, :]

    def entry(a, j):
        if j == a // 2 and a % 2 == 1:
            return diagonal
        if j == a // 2 and a == order - 1:
            return jnp.where(low, diagonal, double(3, a))
        square = None
        for c in range(3):
            gap = double(c, a) - single(c, j)
            square = gap * gap if square is None else square + gap * gap
        distance = square * lax.rsqrt(jnp.maximum(square, 1e-35))
        value = (1.0 + distance) * jnp.exp2(distance * minus_log2_e)
        if j == a // 2:
            value = jnp.where(low, diagonal, value)
        if j == pairs - 1:
            value = jnp.where(low, value, double(3, a))
        return value

    def halves(value):
        other = pltpu.roll(value, groups, 0)
        return jnp.where(low, value, other), jnp.where(low, other, value)

    def final_at(k, j):
        return pl.ds((k * pairs + j) * SUBLANES, SUBLANES)

    def scaled_at(k, a):
        return pl.ds((k * order + a) * SUBLANES, SUBLANES)

    block = 4

    def eliminate(p, waiting):
        columns = range(p * SUBLANES // 2, (p + 1) * SUBLANES // 2)
        start = p * SUBLANES
        tops = range(0, min(start + SUBLANES, order), block)
        for step, top in enumerate(tops):
            for part in waiting[step * len(waiting) // len(tops) : (step + 1) * len(waiting) // len(tops)]:
                gather(*part)
            rows = range(top, min(top + block, order))
            held = {(a, j): entry(a, j) for a in rows for j in columns if j >= a // 2}
            for k in range(top):
                factors = {a: scaled[scaled_at(k, a), :] for a in rows}
                for j in columns:
                    row = final[final_at(k, j), :]
                    for a in rows:
                        if j >= a // 2:
                            held[a, j] = held[a, j] - factors[a] * row
            made = {}
            for a in rows:
                for k in range(top, a):
                    factor = made[k, a] if (k, a) in made else scaled[scaled_at(k, a), :]
                    for j in columns:
                        if j >= a // 2:
                            held[a, j] = held[a, j] - factor * held[k, j]
                if a == order - 1:
                    pivot = held[a, pairs - 1]
                    white = pltpu.roll(pivot, groups, 0) * lax.rsqrt(pivot)
                    white_ref[...] = white[:groups]
                    term = jnp.where(low, jnp.log(pivot) + white * white, 0.0)
                    total = jnp.sum(term, axis=0, keepdims=True)
                    part_ref[...] = jnp.broadcast_to(total, part_ref.shape)
                    break
                if a >= start:
                    inverse = 1.0 / halves(held[a, a // 2])[a % 2]
                    inverses[a * SUBLANES : (a + 1) * SUBLANES, :] = inverse
                else:
                    inverse = inverses[a * SUBLANES : (a + 1) * SUBLANES, :]
                for j in columns:
                    if j < a // 2:
                        continue
                    final[final_at(a, j), :] = held[a, j]
                    if 2 * j + 1 <= a:
                        continue
                    pair = halves(held[a, j] * inverse)
                    for half in range(2):
                        m = 2 * j + half
                        if a < m < order:
                            made[a, m] = pair[half]
                            scaled[scaled_at(a, m), :] = pair[half]

    for g in range(groups):
        gather(0, g)
    for p in range(panels):
        eliminate(p, [(p + 1, g) for g in range(groups)] if p + 1 < panels else [])


def finish(parts_ref, white_ref, out_ref, total_ref):
    out_ref[...] = white_ref[...]
    points = parts_ref.shape[0] * white_ref.shape[0] * white_ref.shape[1]
    total = jnp.sum(jnp.sum(parts_ref[...], axis=0, keepdims=True), axis=1, keepdims=True)
    total_ref[...] = total / (2.0 * points) + half_log_tau


def body(coords, observations, length_scales, nugget, fetch_table, slot_of):
    local = coords.shape[1]
    owners, capacity = fetch_table.shape[1:]
    count = slot_of.shape[0]
    groups = local // LANES
    order = count + 1
    pairs = (order + 1) // 2
    panels = pairs * 2 // SUBLANES
    assert 2 * groups == SUBLANES and (order + 1) % SUBLANES == 0
    assert capacity <= LANES and panels * EARLY <= LANES
    devices = lax.axis_size("pts") * lax.axis_size("grp")
    payload = jnp.concatenate([coords, observations[None, :]], axis=0)
    n_slabs = lax.axis_size("grp")
    assert n_slabs % 2 == 0 and devices % (2 * SUBLANES) == 0
    alike = [[d for d in range(devices) if d % 2 == parity] for parity in range(2)]
    same = jnp.broadcast_to(payload[None], (devices // 2, CHANNELS, local))
    same = lax.all_to_all(same, AXES, split_axis=0, concat_axis=0, tiled=True, axis_index_groups=alike)
    same, length_scales, nugget = lax.optimization_barrier((same, length_scales, nugget))
    other = lax.ppermute(same, "grp", [(i, i ^ 1) for i in range(n_slabs)])

    def rows(received):
        received = received.reshape(devices // 2, CHANNELS, groups, LANES).transpose(0, 2, 1, 3)
        return received.reshape(devices // 2 * CHANNELS * groups, LANES)

    scalars = jnp.concatenate([length_scales, nugget])[None]
    vmem = pl.BlockSpec(memory_space=pltpu.VMEM)
    white, part = pl.pallas_call(
        kernel,
        out_shape=(
            jax.ShapeDtypeStruct((groups, LANES), jnp.float32),
            jax.ShapeDtypeStruct((devices, LANES), jnp.float32),
        ),
        in_specs=[vmem] * 5,
        out_specs=(vmem, vmem),
        scratch_shapes=[
            pltpu.VMEM((panels * SUBLANES, local), jnp.int32),
            pltpu.VMEM((owners, LANES), jnp.int32),
            pltpu.VMEM((CHANNELS, owners, LANES), jnp.float32),
            pltpu.VMEM((3, pairs * SUBLANES, LANES), jnp.float32),
            pltpu.VMEM((CHANNELS, 2 * pairs * SUBLANES, LANES), jnp.float32),
            pltpu.VMEM((order * pairs * SUBLANES, LANES), jnp.float32),
            pltpu.VMEM((order * order * SUBLANES, LANES), jnp.float32),
            pltpu.VMEM((order * SUBLANES, LANES), jnp.float32),
        ],
        compiler_params=pltpu.CompilerParams(vmem_limit_bytes=16 << 20),
    )(rows(same), rows(other), slot_of, fetch_table[0], scalars)
    parts = lax.all_to_all(part, AXES, split_axis=0, concat_axis=0, tiled=True)
    white, neg_loglik = pl.pallas_call(
        finish,
        out_shape=(
            jax.ShapeDtypeStruct((groups, LANES), jnp.float32),
            jax.ShapeDtypeStruct((1, 1), jnp.float32),
        ),
        in_specs=[vmem, vmem],
        out_specs=(vmem, vmem),
        compiler_params=pltpu.CompilerParams(vmem_limit_bytes=1 << 20),
    )(parts, white)
    return (white.reshape(local), neg_loglik[0, 0])


def solution(mesh):
    in_specs = (P(None, AXES), P(AXES), P(), P(), P(AXES, None, None), P(None, AXES))
    out_specs = (P(AXES), P())
    return jax.shard_map(body, mesh=mesh, in_specs=in_specs, out_specs=out_specs, check_vma=False)
```

```python
import jax
import jax.numpy as jnp
from jax import lax
from jax.experimental import pallas as pl
from jax.experimental.pallas import tpu as pltpu
from jax.sharding import PartitionSpec as P

root_three = 1.7320508075688772
minus_log2_e = -1.4426950408889634
half_log_tau = 0.9189385332046727
LANES = 128
SUBLANES = 8
CHANNELS = 4
EARLY = 32
AXES = ("pts", "grp")


def lane_gather(row, index):
    return jnp.take_along_axis(row, index, axis=1, mode="promise_in_bounds")


def tile_of(ref, row):
    return jnp.broadcast_to(ref[pl.ds(row, 1), :], (SUBLANES, LANES))


def kernel(same_ref, other_ref, slot_ref, table_ref, scalars, white_ref, part_ref,
           slots, far_index, far_rows, singles, doubles, final, scaled, inverses):
    owners, capacity = table_ref.shape
    count, local = slot_ref.shape
    groups = local // LANES
    rows_each = CHANNELS * groups
    near_slots = 3 * local
    order = count + 1
    pairs = (order + 1) // 2
    panels = pairs * 2 // SUBLANES
    full = (SUBLANES, LANES)
    tile_id, slab_id = lax.axis_index("pts"), lax.axis_index("grp")
    n_tiles, n_slabs = lax.axis_size("pts"), lax.axis_size("grp")
    device = tile_id * n_slabs + slab_id
    scales = [root_three / jnp.broadcast_to(scalars[:, c : c + 1], full) for c in range(3)]
    low = lax.broadcasted_iota(jnp.int32, full, 0) < groups
    lane_id = lax.broadcasted_iota(jnp.int32, full, 1)
    diagonal = 1.0 + jnp.broadcast_to(scalars[:, 3:4], full)

    far_index[...] = jnp.zeros(far_index.shape, jnp.int32)
    far_index[:, :capacity] = table_ref[...]
    parity = device % 2
    for start, first, ref, base in [
        (start, first, ref, base)
        for start, first, ref in ((0, parity, same_ref), (owners // 2, 1 - parity, other_ref))
        for base in range(0, owners // 2, SUBLANES)
    ]:
        index = far_index[pl.ds(first + 2 * base, SUBLANES, stride=2), :]
        lane, chunk = index & (LANES - 1), index >> 7
        for c in range(CHANNELS):
            value = None
            for g in range(groups):
                source = ref[pl.ds(base * rows_each + g * CHANNELS + c, SUBLANES, stride=rows_each), :]
                picked = lane_gather(source, lane)
                value = picked if value is None else jnp.where(chunk == g, picked, value)
            far_rows[c, start + base : start + base + SUBLANES, :] = value

    slots[count:, :] = jnp.zeros((slots.shape[0] - count, local), jnp.int32)
    slots[:count, :] = slot_ref[...]

    packed = slots[:SUBLANES, :LANES]
    for p in range(1, panels):
        moved = pltpu.roll(slots[p * SUBLANES : (p + 1) * SUBLANES, :LANES], p * EARLY, 1)
        packed = jnp.where(lane_id < p * EARLY, packed, moved)
    far = [jnp.zeros(full, jnp.float32)] * CHANNELS
    for o in range(owners):
        if o % (owners // 2) == 0:
            place = packed - near_slots - capacity * (parity if o == 0 else 1 - parity)
        here = (place >= 0) & (place < capacity)
        lane = place & (LANES - 1)
        for c in range(CHANNELS):
            far[c] = jnp.where(here, lane_gather(tile_of(far_rows.at[c], o), lane), far[c])
        place = place - 2 * capacity

    neighbours = [
        (jnp.maximum(tile_id - 1, 0) * n_slabs + slab_id) // 2,
        device // 2,
        (jnp.minimum(tile_id + 1, n_tiles - 1) * n_slabs + slab_id) // 2,
    ]

    def gather(p, g):
        first = p * SUBLANES
        mine = slots[first : first + SUBLANES, g * LANES : (g + 1) * LANES]
        lane, chunk = mine & (LANES - 1), mine >> 7
        found = [None] * CHANNELS
        for t in range(3):
            for q in range(groups):
                here = chunk == t * groups + q
                for c in range(CHANNELS):
                    picked = lane_gather(tile_of(same_ref, neighbours[t] * rows_each + q * CHANNELS + c), lane)
                    found[c] = picked if found[c] is None else jnp.where(here, picked, found[c])
        if g == 0:
            distant = mine >= near_slots
            for c in range(CHANNELS):
                moved = pltpu.roll(far[c], LANES - p * EARLY, 1) if p else far[c]
                found[c] = jnp.where(distant, moved, found[c])
        for c in range(CHANNELS):
            value = found[c]
            if c < 3:
                value = value * scales[c]
                singles[c, pl.ds(first * groups + g, SUBLANES, stride=groups), :] = value
            for half in range(2):
                start = first * SUBLANES + half * groups + g
                doubles[c, pl.ds(start, SUBLANES, stride=SUBLANES), :] = value
        if p == panels - 1 and g == groups - 1:
            for c in range(CHANNELS):
                own = same_ref[pl.ds(device // 2 * rows_each + c, groups, stride=CHANNELS), :]
                if c < 3:
                    own = own * scales[c][:groups]
                    singles[c, count * groups : (count + 1) * groups, :] = own
                for half in range(2):
                    start = count * SUBLANES + half * groups
                    doubles[c, start : start + groups, :] = own

    def single(c, j):
        return singles[c, j * SUBLANES : (j + 1) * SUBLANES, :]

    def double(c, a):
        return doubles[c, a * SUBLANES : (a + 1) * SUBLANES, :]

    def entry(a, j):
        if j == a // 2 and a % 2 == 1:
            return diagonal
        if j == a // 2 and a == order - 1:
            return jnp.where(low, diagonal, double(3, a))
        square = None
        for c in range(3):
            gap = double(c, a) - single(c, j)
            square = gap * gap if square is None else square + gap * gap
        distance = square * lax.rsqrt(jnp.maximum(square, 1e-35))
        value = (1.0 + distance) * jnp.exp2(distance * minus_log2_e)
        if j == a // 2:
            value = jnp.where(low, diagonal, value)
        if j == pairs - 1:
            value = jnp.where(low, value, double(3, a))
        return value

    def halves(value):
        other = pltpu.roll(value, groups, 0)
        return jnp.where(low, value, other), jnp.where(low, other, value)

    def final_at(k, j):
        return pl.ds((k * pairs + j) * SUBLANES, SUBLANES)

    def scaled_at(k, a):
        return pl.ds((k * order + a) * SUBLANES, SUBLANES)

    block = 4

    def eliminate(p, waiting):
        columns = range(p * SUBLANES // 2, (p + 1) * SUBLANES // 2)
        start = p * SUBLANES
        tops = range(0, min(start + SUBLANES, order), block)
        for step, top in enumerate(tops):
            for part in waiting[step * len(waiting) // len(tops) : (step + 1) * len(waiting) // len(tops)]:
                gather(*part)
            rows = range(top, min(top + block, order))
            held = {(a, j): entry(a, j) for a in rows for j in columns if j >= a // 2}
            for k in range(top):
                factors = {a: scaled[scaled_at(k, a), :] for a in rows}
                for j in columns:
                    row = final[final_at(k, j), :]
                    for a in rows:
                        if j >= a // 2:
                            held[a, j] = held[a, j] - factors[a] * row
            made = {}
            for a in rows:
                for k in range(top, a):
                    factor = made[k, a] if (k, a) in made else scaled[scaled_at(k, a), :]
                    for j in columns:
                        if j >= a // 2:
                            held[a, j] = held[a, j] - factor * held[k, j]
                if a == order - 1:
                    pivot = held[a, pairs - 1]
                    white = pltpu.roll(pivot, groups, 0) * lax.rsqrt(pivot)
                    white_ref[...] = white[:groups]
                    term = jnp.where(low, jnp.log(pivot) + white * white, 0.0)
                    total = jnp.sum(term, axis=0, keepdims=True)
                    part_ref[...] = jnp.broadcast_to(total, part_ref.shape)
                    break
                if a >= start:
                    inverse = 1.0 / halves(held[a, a // 2])[a % 2]
                    inverses[a * SUBLANES : (a + 1) * SUBLANES, :] = inverse
                else:
                    inverse = inverses[a * SUBLANES : (a + 1) * SUBLANES, :]
                for j in columns:
                    if j < a // 2:
                        continue
                    final[final_at(a, j), :] = held[a, j]
                    if 2 * j + 1 <= a:
                        continue
                    pair = halves(held[a, j] * inverse)
                    for half in range(2):
                        m = 2 * j + half
                        if a < m < order:
                            made[a, m] = pair[half]
                            scaled[scaled_at(a, m), :] = pair[half]

    for g in range(groups):
        gather(0, g)
    for p in range(panels):
        eliminate(p, [(p + 1, g) for g in range(groups)] if p + 1 < panels else [])


def finish(parts_ref, white_ref, out_ref, total_ref):
    out_ref[...] = white_ref[...]
    points = parts_ref.shape[0] * white_ref.shape[0] * white_ref.shape[1]
    total = jnp.sum(jnp.sum(parts_ref[...], axis=0, keepdims=True), axis=1, keepdims=True)
    total_ref[...] = total / (2.0 * points) + half_log_tau


def body(coords, observations, length_scales, nugget, fetch_table, slot_of):
    local = coords.shape[1]
    owners, capacity = fetch_table.shape[1:]
    count = slot_of.shape[0]
    groups = local // LANES
    order = count + 1
    pairs = (order + 1) // 2
    panels = pairs * 2 // SUBLANES
    assert 2 * groups == SUBLANES and (order + 1) % SUBLANES == 0
    assert capacity <= LANES and panels * EARLY <= LANES
    devices = lax.axis_size("pts") * lax.axis_size("grp")
    payload = jnp.concatenate([coords, observations[None, :]], axis=0)
    n_slabs = lax.axis_size("grp")
    assert n_slabs % 2 == 0 and devices % (2 * SUBLANES) == 0
    alike = [[d for d in range(devices) if d % 2 == parity] for parity in range(2)]
    same = jnp.broadcast_to(payload[None], (devices // 2, CHANNELS, local))
    same = lax.all_to_all(same, AXES, split_axis=0, concat_axis=0, tiled=True, axis_index_groups=alike)
    same, length_scales, nugget = lax.optimization_barrier((same, length_scales, nugget))
    other = lax.ppermute(same, "grp", [(i, i ^ 1) for i in range(n_slabs)])

    def rows(received):
        received = received.reshape(devices // 2, CHANNELS, groups, LANES).transpose(0, 2, 1, 3)
        return received.reshape(devices // 2 * CHANNELS * groups, LANES)

    scalars = jnp.concatenate([length_scales, nugget])[None]
    vmem = pl.BlockSpec(memory_space=pltpu.VMEM)
    white, part = pl.pallas_call(
        kernel,
        out_shape=(
            jax.ShapeDtypeStruct((groups, LANES), jnp.float32),
            jax.ShapeDtypeStruct((devices, LANES), jnp.float32),
        ),
        in_specs=[vmem] * 5,
        out_specs=(vmem, vmem),
        scratch_shapes=[
            pltpu.VMEM((panels * SUBLANES, local), jnp.int32),
            pltpu.VMEM((owners, LANES), jnp.int32),
            pltpu.VMEM((CHANNELS, owners, LANES), jnp.float32),
            pltpu.VMEM((3, pairs * SUBLANES, LANES), jnp.float32),
            pltpu.VMEM((CHANNELS, 2 * pairs * SUBLANES, LANES), jnp.float32),
            pltpu.VMEM((order * pairs * SUBLANES, LANES), jnp.float32),
            pltpu.VMEM((order * order * SUBLANES, LANES), jnp.float32),
            pltpu.VMEM((order * SUBLANES, LANES), jnp.float32),
        ],
        compiler_params=pltpu.CompilerParams(vmem_limit_bytes=16 << 20),
    )(rows(same), rows(other), slot_of, fetch_table[0], scalars)
    parts = lax.all_to_all(part, AXES, split_axis=0, concat_axis=0, tiled=True)
    white, neg_loglik = pl.pallas_call(
        finish,
        out_shape=(
            jax.ShapeDtypeStruct((groups, LANES), jnp.float32),
            jax.ShapeDtypeStruct((1, 1), jnp.float32),
        ),
        in_specs=[vmem, vmem],
        out_specs=(vmem, vmem),
        compiler_params=pltpu.CompilerParams(vmem_limit_bytes=1 << 20),
    )(parts, white)
    return (white.reshape(local), neg_loglik[0, 0])


def solution(mesh):
    in_specs = (P(None, AXES), P(AXES), P(), P(), P(AXES, None, None), P(None, AXES))
    out_specs = (P(AXES), P())
    return jax.shard_map(body, mesh=mesh, in_specs=in_specs, out_specs=out_specs, check_vma=False)
```
